256 devices in a mesh: dp: 16 (over y_lo, z), expert: 16 (over y_hi, x, core).
Axes of the slice: x: 4, y: 4 (y_hi: 2, y_lo: 2; y = y_hi * 2 + y_lo), z: 8, core: 2. Of those that a mesh axis runs over, the one named last changes fastest.
Arguments:
- tokens: bfloat16 [32768, 2560], P(('dp', 'expert')), may hold values from -6 to 6
- routing: int32 [32768, 6], P(('dp', 'expert')), may hold values from 0 to 15, as said below
- gates: float32 [32768, 6], P(('dp', 'expert')), may hold values from 0.1 to 1
- cotangent: bfloat16 [32768, 2560], P(('dp', 'expert')), may hold values from -0.29882812 to 0.29882812
- w_in: bfloat16 [16, 2560, 768], P('expert'), may hold values from -0.125 to 0.125
- w_out: bfloat16 [16, 768, 2560], P('expert'), may hold values from -0.21875 to 0.21875
Outputs:
- grad_in: float32 [16, 2560, 768], P('expert', 'dp')
- grad_out: float32 [16, 768, 2560], P('expert', 'dp')
The draws below stay inside these ranges and needn't reach their ends.
Inputs may be any that keep to these rules, and one draw needn't show every extreme that they name: `routing`: each row names 6 different experts.
All inputs are finite; a program needn't handle non-finite values.
Results may differ from the reference program's by a relative error of at most 0.0055.
Values may be sent and summed in bfloat16 or wider, within the bound.
A program may use at most 128 MiB of HBM per device.

```python
import math
import jax
import jax.numpy as jnp
from jax import lax

D = 2560
FF = 768
TOK_DEV = 128
EXPERTS = 16
TOPK = 6
CAP = 40
TOKENS = 32768
N_DP = 16
N_EXPERT = 16


def expert_ranks(key):
    hot_expert = jax.random.randint(jax.random.fold_in(key, 7), (), 0, EXPERTS, dtype=jnp.int32)
    cold_expert = (hot_expert + EXPERTS // 2) % EXPERTS
    others = jax.random.permutation(jax.random.fold_in(key, 11), EXPERTS - 2).astype(jnp.int32) + 1
    labels = jnp.arange(EXPERTS, dtype=jnp.int32)
    position = labels - (labels > hot_expert).astype(jnp.int32) - (labels > cold_expert).astype(jnp.int32)
    position = jnp.clip(position, 0, EXPERTS - 3)
    middle = others[position]
    return jnp.where(labels == hot_expert, EXPERTS - 1, jnp.where(labels == cold_expert, 0, middle)).astype(jnp.int32)


def draw_routing(key, part):
    ranks = expert_ranks(key)
    noise = jax.random.randint(jax.random.fold_in(key, 23), (TOKENS, EXPERTS), 0, 65536, dtype=jnp.int32)
    scores = (noise + ranks[None, :] * 1536) * EXPERTS + jnp.arange(EXPERTS, dtype=jnp.int32)[None, :]
    _, chosen = lax.top_k(scores, TOPK)
    return chosen.astype(jnp.int32)


def steps_of(stream_key, shape, cuts, least, largest):
    def one(axis_at, shards_of):
        steps = jax.random.uniform(jax.random.fold_in(jax.random.fold_in(stream_key, 6), axis_at), (shards_of,), jnp.float32, least / len(cuts), largest / len(cuts))
        return jnp.repeat(jnp.exp(steps), shape[axis_at] // shards_of).reshape((-1,) + (1,) * (len(shape) - axis_at - 1))

    factor_of = one(*cuts[0])
    for cut in cuts[1:]:
        factor_of = factor_of * one(*cut)
    return factor_of


def gaussian(own_key, shape, spread, reach, pieces=(), kind=jnp.bfloat16):
    result = spread * jax.random.normal(own_key, shape, jnp.float32)
    if pieces:
        result = result * steps_of(own_key, shape, pieces, -0.22, 0.18)
    return jnp.clip(result, -reach, reach).astype(kind)


def setup_inputs(seed: int = 0) -> dict:
    keys = jax.random.split(jax.random.key(seed), 7)
    tokens = gaussian(keys[0], (TOKENS, D), 1.0, 6.0, ((0, 256),))
    routing = draw_routing(jax.random.fold_in(keys[6], 71), 0)
    gates = jnp.clip(jnp.exp(math.log(1.0) - 2.3025851 * jax.random.uniform(keys[2], (TOKENS, TOPK), jnp.float32) ** steps_of(keys[2], (TOKENS, TOPK), ((0, 256),), -0.2, 0.2)), 0.1, 1.0)
    cotangent = gaussian(keys[3], (TOKENS, D), 0.05, 0.29882812, ((0, 256),))
    w_in = gaussian(keys[4], (EXPERTS, D, FF), D ** -0.5, 0.125, ((0, 16),))
    w_out = gaussian(keys[5], (EXPERTS, FF, D), FF ** -0.5, 0.21875, ((0, 16),))
    return dict(tokens=tokens, routing=routing, gates=gates, cotangent=cotangent, w_in=w_in, w_out=w_out)


def silu_slope(values):
    sigma = jax.nn.sigmoid(values)
    return sigma * (1.0 + values * (1.0 - sigma))


def slot_table(chosen):
    entries = chosen.shape[0]
    onehot = (chosen[:, None] == jnp.arange(EXPERTS, dtype=jnp.int32)[None, :]).astype(jnp.int32)
    earlier = jnp.cumsum(onehot, axis=0) - onehot
    rank_of = jnp.sum(earlier * onehot, axis=1).astype(jnp.int32)
    target = jnp.where(rank_of < CAP, chosen * CAP + rank_of, EXPERTS * CAP).astype(jnp.int32)
    filled = jnp.full((EXPERTS * CAP,), entries, jnp.int32)
    filled = filled.at[target].set(jnp.arange(entries, dtype=jnp.int32), mode="drop")
    return filled.reshape(EXPERTS, CAP)


def pick_rows(source, index):
    return source[index]


def reference(tokens, routing, gates, cotangent, w_in, w_out):
    entries = TOK_DEV * TOPK
    token_blocks = tokens.reshape(N_DP, N_EXPERT, TOK_DEV, D)
    route_blocks = routing.reshape(N_DP, N_EXPERT, entries)
    gate_blocks = gates.reshape(N_DP, N_EXPERT, entries)
    cot_blocks = cotangent.reshape(N_DP, N_EXPERT, TOK_DEV, D)

    def one_row(totals, dp_block):
        row_tokens, row_routes, row_gates, row_cots = dp_block
        tables = jax.vmap(slot_table)(row_routes)
        padded_tokens = jnp.concatenate([row_tokens, jnp.zeros((N_EXPERT, 1, D), row_tokens.dtype)], axis=1)
        padded_cots = jnp.concatenate([row_cots, jnp.zeros((N_EXPERT, 1, D), row_cots.dtype)], axis=1)
        padded_gates = jnp.concatenate([row_gates, jnp.zeros((N_EXPERT, 1), row_gates.dtype)], axis=1)

        def one_expert(expert):
            table = tables[:, expert, :]
            token_of = (table // TOPK).astype(jnp.int32)
            rows_in = jax.vmap(pick_rows)(padded_tokens, token_of).reshape(-1, D)
            rows_cot = jax.vmap(pick_rows)(padded_cots, token_of).reshape(-1, D)
            row_gates = jax.vmap(pick_rows)(padded_gates, table).reshape(-1)
            scaled = (rows_cot.astype(jnp.float32) * row_gates[:, None]).astype(jnp.bfloat16)
            weight_in = w_in[expert]
            weight_out = w_out[expert]
            pre_act = jnp.dot(rows_in, weight_in, preferred_element_type=jnp.float32)
            hidden = jax.nn.silu(pre_act).astype(jnp.bfloat16)
            back_grad = jnp.dot(scaled, weight_out.T, preferred_element_type=jnp.float32)
            pre_grad = (back_grad * silu_slope(pre_act)).astype(jnp.bfloat16)
            part_out = jnp.dot(hidden.T, scaled, preferred_element_type=jnp.float32).astype(jnp.bfloat16)
            part_in = jnp.dot(rows_in.T, pre_grad, preferred_element_type=jnp.float32).astype(jnp.bfloat16)
            return part_in, part_out

        part_in, part_out = lax.map(one_expert, jnp.arange(EXPERTS, dtype=jnp.int32))
        part_in, part_out = lax.optimization_barrier((part_in, part_out))
        return (totals[0] + part_in.astype(jnp.float32), totals[1] + part_out.astype(jnp.float32)), None

    start = (jnp.zeros((EXPERTS, D, FF), jnp.float32), jnp.zeros((EXPERTS, FF, D), jnp.float32))
    sums, _ = lax.scan(one_row, start, (token_blocks, route_blocks, gate_blocks, cot_blocks))
    return sums[0], sums[1]
```

```python
import jax
import jax.numpy as jnp
from jax import lax
from jax.sharding import PartitionSpec as P


def silu_slope(values):
    sigma = jax.nn.sigmoid(values)
    return sigma * (1.0 + values * (1.0 - sigma))


def forward_rows(rows_in, weight_in):
    pre_act = jnp.dot(rows_in, weight_in, preferred_element_type=jnp.float32)
    return (pre_act, jax.nn.silu(pre_act).astype(jnp.bfloat16))


def backward_rows(rows_grad, weight_out, pre_act):
    back_grad = lax.dot_general(
        rows_grad, weight_out, (((1,), (1,)), ((), ())), preferred_element_type=jnp.float32
    )
    return (back_grad * silu_slope(pre_act)).astype(jnp.bfloat16)


def outer_sums(rows_in, rows_grad, hidden, pre_grad):
    grad_o = lax.dot_general(
        hidden, rows_grad, (((0,), (0,)), ((), ())), preferred_element_type=jnp.float32
    )
    grad_i = lax.dot_general(
        rows_in, pre_grad, (((0,), (0,)), ((), ())), preferred_element_type=jnp.float32
    )
    return (grad_i, grad_o)


def body(tokens, routing, gates, cotangent, w_in, w_out):
    peer_count = lax.axis_size("expert")
    tok_count = tokens.shape[0]
    top_count = routing.shape[1]
    width_model = tokens.shape[1]
    hidden_width = w_in.shape[2]
    entries = tok_count * top_count
    capacity = tok_count * top_count * 5 // (peer_count * 6)
    chosen = routing.reshape(entries)
    onehot = (chosen[:, None] == jnp.arange(peer_count, dtype=jnp.int32)[None, :]).astype(jnp.int32)
    earlier = jnp.cumsum(onehot, axis=0) - onehot
    rank_of = jnp.sum(earlier * onehot, axis=1)
    target = jnp.where(rank_of < capacity, chosen * capacity + rank_of, peer_count * capacity)
    slot_entry = jnp.full((peer_count * capacity,), entries, jnp.int32)
    slot_entry = slot_entry.at[target].set(jnp.arange(entries, dtype=jnp.int32), mode="drop")
    token_of = slot_entry // top_count
    padded_tokens = jnp.concatenate([tokens, jnp.zeros((1, width_model), tokens.dtype)], axis=0)
    padded_cots = jnp.concatenate([cotangent, jnp.zeros((1, width_model), cotangent.dtype)], axis=0)
    padded_gates = jnp.concatenate([gates.reshape(entries), jnp.zeros((1,), jnp.float32)], axis=0)
    sent_inputs = padded_tokens[token_of].reshape(peer_count, capacity, width_model)
    sent_grads = (
        padded_cots[token_of].astype(jnp.float32) * padded_gates[slot_entry][:, None]
    ).astype(jnp.bfloat16)
    sent_grads = sent_grads.reshape(peer_count, capacity, width_model)
    weight_in = w_in[0]
    weight_out = w_out[0]
    got_inputs, got_grads = (
        lax.all_to_all(sent_inputs, "expert", split_axis=0, concat_axis=0, tiled=True),
        lax.all_to_all(sent_grads, "expert", split_axis=0, concat_axis=0, tiled=True),
    )
    rows_in = got_inputs.reshape(peer_count * capacity, width_model)
    rows_grad = got_grads.reshape(peer_count * capacity, width_model)
    pre_act, hidden = forward_rows(rows_in, weight_in)
    pre_grad = backward_rows(rows_grad, weight_out, pre_act)
    part_in, part_out = outer_sums(rows_in, rows_grad, hidden, pre_grad)
    rounded_in = part_in.astype(jnp.bfloat16)
    rounded_out = part_out.astype(jnp.bfloat16)
    sum_in = lax.psum_scatter(rounded_in, "dp", scatter_dimension=0, tiled=True).astype(jnp.float32)
    sum_out = lax.psum_scatter(rounded_out, "dp", scatter_dimension=0, tiled=True).astype(jnp.float32)
    return (sum_in[None], sum_out[None])


def solution(mesh):
    in_specs = (
        P(("dp", "expert"), None),
        P(("dp", "expert"), None),
        P(("dp", "expert"), None),
        P(("dp", "expert"), None),
        P("expert", None, None),
        P("expert", None, None),
    )
    out_specs = (P("expert", "dp", None), P("expert", "dp", None))
    return jax.shard_map(body, mesh=mesh, in_specs=in_specs, out_specs=out_specs, check_vma=False)
```

```python
import functools

import jax
import jax.numpy as jnp
from jax import lax
from jax.experimental import pallas as pl
from jax.experimental.pallas import tpu as pltpu
from jax.sharding import PartitionSpec as P

MESH = pl.DeviceIdType.MESH
BF = jnp.bfloat16
F32 = jnp.float32
NEX = 16
CAP = 40
ROWS = NEX * CAP
TOK_SPLIT = 2
COT_SPLIT = 4
IN_UNITS = 3
RING = 8
HOPS = [(0, 1, 0)] + [(0, s, p) for s in (2, 3, 4) for p in (0, 1)]
HOPS += [(1, 1, 1)] + [(1, s, p) for s in (2, 3, 4) for p in (0, 1)]
HOP = {hop: i for i, hop in enumerate(HOPS)}


def silu_slope(values):
    sigma = jax.nn.sigmoid(values)
    return sigma * (1.0 + values * (1.0 - sigma))


def mm(a, b, dims):
    return lax.dot_general(a, b, (dims, ((), ())), preferred_element_type=F32)


def kernel(routing, gates, tok, cot, win_hbm, wout_hbm, gin, gout,
           win, wout, stok, scot, rtok, rcot, tokf, cotb, onehot, pre, slope, back, hid, pgrad,
           po, pi, rzo, rzi, yso, yro, ysi, yri,
           wsem, lsem, ts, tr, cs, cr, zos, zor, zis, zir, yos, yor, yis, yir):
    me = lax.axis_index("expert")
    dp = lax.axis_index("dp")
    yl = dp // RING
    z = lax.rem(dp, RING)
    up = {"dp": yl * RING + lax.rem(z + 1, RING)}
    down = {"dp": yl * RING + lax.rem(z + RING - 1, RING)}
    side = {"dp": (1 - yl) * RING + z}
    width = tok.shape[1]
    toks = tok.shape[0]

    copies = []
    for i, (src, dst) in enumerate(((win_hbm, win), (wout_hbm, wout))):
        copy = pltpu.make_async_copy(src.at[0], dst, wsem.at[i])
        copy.start()
        copies.append(copy)

    barrier = pltpu.get_barrier_semaphore()
    for o in range(1, NEX):
        pl.semaphore_signal(barrier, inc=1, device_id={"expert": lax.rem(me + o, NEX)}, device_id_type=MESH)
    for peer in (up, down, side):
        pl.semaphore_signal(barrier, inc=1, device_id=peer, device_id_type=MESH)

    expert = lax.broadcasted_iota(jnp.int32, (NEX, toks), 0)
    member = jnp.zeros((NEX, toks), F32)
    weight = jnp.zeros((NEX, toks), F32)
    for k in range(routing.shape[0]):
        hit = routing[k : k + 1, :] == expert
        member = jnp.where(hit, 1.0, member)
        weight = jnp.where(hit, gates[k : k + 1, :], weight)
    before = lax.broadcasted_iota(jnp.int32, (toks, toks), 0) < lax.broadcasted_iota(jnp.int32, (toks, toks), 1)
    rank = mm(member.astype(BF), jnp.where(before, 1.0, 0.0).astype(BF), ((1,), (0,)))
    rank = jnp.where(member > 0.0, rank, -1.0)
    place = lax.broadcasted_iota(jnp.int32, (NEX, CAP, toks), 1).astype(F32)
    match = place == rank[:, None, :]
    onehot[...] = jnp.where(match, 1.0, 0.0).reshape(ROWS, toks).astype(BF)
    gate = jnp.sum(jnp.where(match, weight[:, None, :], 0.0), axis=2, keepdims=True).reshape(ROWS, 1)

    pl.semaphore_wait(barrier, NEX + 2)

    def dispatch(source, send, recv, ssem, rsem, splits, which, scale):
        size = width // splits
        out = []
        for k in range(splits):
            step = 256 if size % 256 == 0 else 128
            for c in range(k * size, (k + 1) * size, step):
                value = mm(onehot[...], source[:, c : c + step], ((1,), (0,)))
                if scale is not None:
                    value = value * scale
                send[:, :, c : c + step] = value.reshape(NEX, CAP, step).astype(BF)
            span = pl.ds(k * size, size)
            row = []
            for o in range(1, NEX):
                target = lax.rem(me + o, NEX)
                copy = pltpu.make_async_remote_copy(
                    src_ref=send.at[target, :, span], dst_ref=recv.at[me, :, span],
                    send_sem=ssem.at[k, o - 1], recv_sem=rsem.at[k, o - 1],
                    device_id={"expert": target}, device_id_type=MESH)
                copy.start()
                row.append(copy)
            own = pltpu.make_async_copy(send.at[me, :, span], recv.at[me, :, span], lsem.at[which, k])
            own.start()
            out.append((row, own))
        return out

    tok_copies = dispatch(tok, stok, rtok, ts, tr, TOK_SPLIT, 0, None)
    cot_copies = dispatch(cot, scot, rcot, cs, cr, COT_SPLIT, 1, gate)

    def arrived(entry):
        row, own = entry
        own.wait()
        for copy in row:
            copy.wait_recv()

    def pieces(distance):
        d = lax.rem(z + distance + RING, RING)
        return ((1 - yl) * RING + d, yl * RING + d)

    def unit_copy(part, landing, ssem, rsem, u, direction, s, p):
        d = 5 - s if direction == 0 else s - 5
        hop = HOP[(direction, s, p)]
        return pltpu.make_async_remote_copy(
            src_ref=part.at[u, pieces(d)[p]], dst_ref=landing.at[u, hop],
            send_sem=ssem.at[u, hop], recv_sem=rsem.at[u, hop],
            device_id=up if direction == 0 else down, device_id_type=MESH)

    def ring_step(group, u, s):
        part, landing, ssem, rsem = group[:4]
        for p in (0, 1):
            for direction in (0, 1):
                if (direction, s, p) not in HOP:
                    continue
                if (direction, s - 1, p) in HOP:
                    unit_copy(part, landing, ssem, rsem, u, direction, s - 1, p).wait_recv()
                    index = pieces(5 - s if direction == 0 else s - 5)[p]
                    got = landing[u, HOP[(direction, s - 1, p)]].astype(F32)
                    part[u, index] = (part[u, index].astype(F32) + got).astype(BF)
                unit_copy(part, landing, ssem, rsem, u, direction, s, p).start()

    def side_copy(group, u):
        ysend, yrecv, yssem, yrsem = group[4:8]
        return pltpu.make_async_remote_copy(
            src_ref=ysend.at[u], dst_ref=yrecv.at[u], send_sem=yssem.at[u], recv_sem=yrsem.at[u],
            device_id=side, device_id_type=MESH)

    def ring_end(group, u):
        part, landing, ssem, rsem = group[:4]
        ysend, out, cols = group[4], group[8], group[9]
        for p in (0, 1):
            for direction in (0, 1):
                unit_copy(part, landing, ssem, rsem, u, direction, 4, p).wait_recv()
            total = part[u, pieces(0)[p]].astype(F32)
            total += landing[u, HOP[(0, 4, p)]].astype(F32) + landing[u, HOP[(1, 4, p)]].astype(F32)
            if p == 0:
                ysend[u] = total.astype(BF)
                side_copy(group, u).start()
            else:
                out[0, :, cols * u : cols * (u + 1)] = total

    def finish(group, u):
        part, landing, ssem, rsem = group[:4]
        yrecv, out, cols = group[5], group[8], group[9]
        side_copy(group, u).wait()
        out[0, :, cols * u : cols * (u + 1)] += yrecv[u].astype(F32)
        for direction, s, p in HOPS:
            unit_copy(part, landing, ssem, rsem, u, direction, s, p).wait_send()

    ff = win.shape[1]
    cblock = width // COT_SPLIT
    iblock = ff // IN_UNITS
    gro = (po, rzo, zos, zor, yso, yro, yos, yor, gout, cblock)
    gri = (pi, rzi, zis, zir, ysi, yri, yis, yir, gin, iblock)

    copies[0].wait()
    tblock = width // TOK_SPLIT
    for k in range(TOK_SPLIT):
        arrived(tok_copies[k])
        span = slice(k * tblock, (k + 1) * tblock)
        for j in range(0, NEX, 2):
            rows = rtok[j : j + 2, :, span].astype(F32).reshape(2 * CAP, tblock)
            tokf[j * CAP : (j + 2) * CAP, span] = rows.astype(BF)
        for n in range(0, ff, 256):
            value = mm(tokf[:, span], win[span, n : n + 256], ((1,), (0,)))
            if k > 0:
                value += pre[:, n : n + 256]
            if k < TOK_SPLIT - 1:
                pre[:, n : n + 256] = value
            else:
                hid[:, n : n + 256] = (value * jax.nn.sigmoid(value)).astype(BF)
                slope[:, n : n + 256] = silu_slope(value)

    copies[1].wait()
    for b in range(COT_SPLIT):
        arrived(cot_copies[b])
        span = slice(b * cblock, (b + 1) * cblock)
        for j in range(0, NEX, 2):
            rows = rcot[j : j + 2, :, span].astype(F32).reshape(2 * CAP, cblock)
            cotb[j * CAP : (j + 2) * CAP, :] = rows.astype(BF)
        for m in range(0, ff, 384):
            value = mm(hid[:, m : m + 384], cotb[...], ((0,), (0,)))
            po[b, m // 48 : (m + 384) // 48] = value.reshape(8, 48, cblock).astype(BF)
        ring_step(gro, b, 1)
        if b >= 1:
            ring_step(gro, b - 1, 3)
        for n in range(0, ff, 256):
            value = mm(cotb[...], wout[n : n + 256, span], ((1,), (1,)))
            if b > 0:
                value += back[:, n : n + 256]
            if b < COT_SPLIT - 1:
                back[:, n : n + 256] = value
            else:
                pgrad[:, n : n + 256] = (value * slope[:, n : n + 256]).astype(BF)
        ring_step(gro, b, 2)
        if b >= 1:
            ring_step(gro, b - 1, 4)
        if b >= 2:
            ring_end(gro, b - 2)

    last = COT_SPLIT - 1
    def part_in(u):
        for m in range(0, width, 640):
            value = mm(tokf[:, m : m + 640], pgrad[:, u * iblock : (u + 1) * iblock], ((0,), (0,)))
            pi[u, m // 160 : (m + 640) // 160] = value.reshape(4, 160, iblock).astype(BF)

    part_in(0)
    ring_step(gri, 0, 1)
    ring_step(gro, last, 3)
    ring_end(gro, last - 1)
    part_in(1)
    ring_step(gri, 1, 1)
    ring_step(gro, last, 4)
    part_in(2)
    ring_step(gri, 2, 1)
    for s in (2, 3, 4):
        for u in range(IN_UNITS):
            ring_step(gri, u, s)
        if s == 2:
            ring_end(gro, last)
    for u in range(IN_UNITS):
        ring_end(gri, u)
    for b in range(COT_SPLIT):
        finish(gro, b)
    for u in range(IN_UNITS):
        finish(gri, u)
    for row, _ in tok_copies + cot_copies:
        for copy in row:
            copy.wait_send()


def body(tokens, routing, gates, cotangent, w_in, w_out):
    width = tokens.shape[1]
    ff = w_in.shape[2]
    cblock = width // COT_SPLIT
    iblock = ff // IN_UNITS
    vmem = pl.BlockSpec(memory_space=pltpu.VMEM)
    hbm = pl.BlockSpec(memory_space=pl.ANY)
    dma = pltpu.SemaphoreType.DMA
    hops = len(HOPS)
    return pl.pallas_call(
        kernel,
        out_shape=(
            jax.ShapeDtypeStruct((1, width // 16, ff), F32),
            jax.ShapeDtypeStruct((1, ff // 16, width), F32),
        ),
        in_specs=[vmem, vmem, vmem, vmem, hbm, hbm],
        out_specs=(vmem, vmem),
        scratch_shapes=[
            pltpu.VMEM((width, ff), BF), pltpu.VMEM((ff, width), BF),
            pltpu.VMEM((NEX, CAP, width), BF), pltpu.VMEM((NEX, CAP, width), BF),
            pltpu.VMEM((NEX, CAP, width), BF), pltpu.VMEM((NEX, CAP, width), BF),
            pltpu.VMEM((ROWS, width), BF), pltpu.VMEM((ROWS, cblock), BF), pltpu.VMEM((ROWS, tokens.shape[0]), BF),
            pltpu.VMEM((ROWS, ff), F32), pltpu.VMEM((ROWS, ff), F32), pltpu.VMEM((ROWS, ff), F32),
            pltpu.VMEM((ROWS, ff), BF), pltpu.VMEM((ROWS, ff), BF),
            pltpu.VMEM((COT_SPLIT, 16, ff // 16, cblock), BF), pltpu.VMEM((IN_UNITS, 16, width // 16, iblock), BF),
            pltpu.VMEM((COT_SPLIT, hops, ff // 16, cblock), BF), pltpu.VMEM((IN_UNITS, hops, width // 16, iblock), BF),
            pltpu.VMEM((COT_SPLIT, ff // 16, cblock), BF), pltpu.VMEM((COT_SPLIT, ff // 16, cblock), BF),
            pltpu.VMEM((IN_UNITS, width // 16, iblock), BF), pltpu.VMEM((IN_UNITS, width // 16, iblock), BF),
            dma((2,)), dma((2, max(TOK_SPLIT, COT_SPLIT))),
            dma((TOK_SPLIT, NEX - 1)), dma((TOK_SPLIT, NEX - 1)),
            dma((COT_SPLIT, NEX - 1)), dma((COT_SPLIT, NEX - 1)),
            dma((COT_SPLIT, hops)), dma((COT_SPLIT, hops)),
            dma((IN_UNITS, hops)), dma((IN_UNITS, hops)),
            dma((COT_SPLIT,)), dma((COT_SPLIT,)), dma((IN_UNITS,)), dma((IN_UNITS,)),
        ],
        compiler_params=pltpu.CompilerParams(
            collective_id=0, has_side_effects=True, vmem_limit_bytes=62 * 1024 * 1024
        ),
    )(routing.T, gates.T, tokens, cotangent, w_in, w_out)


def solution(mesh):
    rows = P(("dp", "expert"), None)
    in_specs = (rows, rows, rows, rows, P("expert", None, None), P("expert", None, None))
    out_specs = (P("expert", "dp", None), P("expert", "dp", None))
    return jax.shard_map(body, mesh=mesh, in_specs=in_specs, out_specs=out_specs, check_vma=False)
```

```python
import functools

import jax
import jax.numpy as jnp
from jax import lax
from jax.experimental import pallas as pl
from jax.experimental.pallas import tpu as pltpu
from jax.sharding import PartitionSpec as P

MESH = pl.DeviceIdType.MESH
BF = jnp.bfloat16
F32 = jnp.float32
NEX = 16
HALF = 8
CAP = 40
ROWS = NEX * CAP
COT_SPLIT = 5
TOK_SPLIT = 2
IN_UNITS = 6
RING = 8
OUT_MODES = "zzzzy"
IN_MODES = "zzzyyy"
PLAN = (
    0, 10, 30, 1, 11, 30, 31, 2, 12, 30, 31, 32, 3, 30, 13, 31, 32, 33, 4, 14, 20, 21, 22, 31, 32,
    33, 40, 41, 42, 32, 34, 33, 40, 41, 42, 34, 43, 33, 40, 41, 44, 42, 43, 34, 40, 41, 44, 45, 42,
    43, 34, 45, 44, 43, 34, 45, 44, 43, 45, 44, 45,
)


def silu_slope(values):
    sigma = jax.nn.sigmoid(values)
    return sigma * (1.0 + values * (1.0 - sigma))


def mm(a, b, dims):
    return lax.dot_general(a, b, (dims, ((), ())), preferred_element_type=F32)


class Sums:
    def __init__(self, modes, cols, out, refs, place):
        self.modes, self.cols, self.out = modes, cols, out
        self.part, self.land, self.ysend, self.yrecv, self.ssem, self.rsem, self.yss, self.yrs = refs
        self.yl, self.z, self.up, self.down, self.side = place
        self.todo = {}

    def hops(self, u, direction):
        return range(1, 5) if self.modes[u] == "z" or u % 2 == direction else range(2, 5)

    def target(self, direction, s):
        return lax.rem(self.z + (5 - s if direction == 0 else s - 5) + RING, RING)

    def piece(self, u, direction, s):
        if self.modes[u] == "y":
            return self.yl
        if s == 1:
            return 1 - self.yl if direction == 0 else self.yl
        return slice(None)

    def remote(self, src, dst, ssem, rsem, device):
        return pltpu.make_async_remote_copy(
            src_ref=src, dst_ref=dst, send_sem=ssem, recv_sem=rsem, device_id=device, device_id_type=MESH)

    def hop(self, u, direction, s):
        slot = direction * 4 + s - 1
        row = self.piece(u, direction, s)
        return self.remote(
            self.part.at[u, row, self.target(direction, s)], self.land.at[u, row, slot],
            self.ssem.at[u], self.rsem.at[u, slot], self.up if direction == 0 else self.down)

    def step(self, u, s):
        for direction in (0, 1):
            if s not in self.hops(u, direction):
                continue
            if s - 1 in self.hops(u, direction):
                self.hop(u, direction, s - 1).wait_recv()
                row = self.piece(u, direction, s - 1)
                at = self.target(direction, s)
                got = self.land[u, row, direction * 4 + s - 2].astype(F32)
                self.part[u, row, at] = (self.part[u, row, at].astype(F32) + got).astype(BF)
            self.hop(u, direction, s).start()

    def ycopy(self, u):
        if self.modes[u] == "y":
            source, target = self.part.at[u, 1 - self.yl], self.land.at[u, self.yl]
        else:
            source, target = self.ysend.at[u], self.yrecv.at[u]
        return self.remote(source, target, self.yss.at[u], self.yrs.at[u], self.side)

    def begin(self, u):
        if self.modes[u] == "y":
            self.ycopy(u).start()
            self.todo[u] = ["add", 2, 3, 4, "end"]
        else:
            self.step(u, 1)
            self.todo[u] = [2, 3, 4, "end"]

    def advance(self, u):
        stage = self.todo[u].pop(0)
        with jax.named_scope(f"{stage}u{u}{self.modes[u]}{self.cols}"):
            if stage == "add":
                self.ycopy(u).wait_recv()
                got = self.land[u, 1 - self.yl].astype(F32)
                self.part[u, self.yl] = (self.part[u, self.yl].astype(F32) + got).astype(BF)
                self.step(u, 1)
            elif stage == "end":
                self.end(u)
            else:
                self.step(u, stage)

    def end(self, u):
        span = slice(self.cols * u, self.cols * (u + 1))
        for direction in (0, 1):
            self.hop(u, direction, 4).wait_recv()
        for row in (1 - self.yl, self.yl) if self.modes[u] == "z" else (self.yl,):
            total = self.part[u, row, self.z].astype(F32)
            total += self.land[u, row, 3].astype(F32) + self.land[u, row, 7].astype(F32)
            if self.modes[u] == "z" and row is not self.yl:
                self.ysend[u] = total.astype(BF)
                self.ycopy(u).start()
            else:
                self.out[0, :, span] = total

    def finish(self, u):
        assert not self.todo[u]
        span = slice(self.cols * u, self.cols * (u + 1))
        copy = self.ycopy(u)
        copy.wait_send()
        sent = slice(0, RING - 1)
        if self.modes[u] == "z":
            copy.wait_recv()
            self.out[0, :, span] += self.yrecv[u].astype(F32)
            all_sent = self.part.at[u, :, sent]
        else:
            all_sent = self.part.at[u, 0, sent]
        self.remote(all_sent, all_sent, self.ssem.at[u], self.rsem.at[u, 0], self.up).wait_send()


def kernel(routing, gates, tok, cot, win_hbm, wout_hbm, gin, gout,
           win, wout, stok, scot, rtok, rcot, tokf, cotb, onehot, prt, pgt, ptok, pcot, slope, back, hid, pgrad,
           po, pi, lo, li, yso, yro, ysi, yri,
           wsem, lsem, ps, pr, ts, tr, cs, cr, zos, zor, zis, zir, yos, yor, yis, yir):
    me = lax.axis_index("expert")
    dp = lax.axis_index("dp")
    yh = me // HALF
    r = lax.rem(me, HALF)
    yl = dp // RING
    z = lax.rem(dp, RING)
    up = {"dp": yl * RING + lax.rem(z + 1, RING)}
    down = {"dp": yl * RING + lax.rem(z + RING - 1, RING)}
    side = {"dp": (1 - yl) * RING + z}
    partner = {"expert": (1 - yh) * HALF + r}
    row = [lax.rem(r + o, HALF) for o in range(HALF)]
    width = tok.shape[1]
    toks = tok.shape[0]
    ff = win.shape[1]
    cblock = width // COT_SPLIT
    iblock = ff // IN_UNITS
    place = (yl, z, up, down, side)
    so = Sums(OUT_MODES, cblock, gout, (po, lo, yso, yro, zos, zor, yos, yor), place)
    si = Sums(IN_MODES, iblock, gin, (pi, li, ysi, yri, zis, zir, yis, yir), place)

    weights = []
    for i, (src, dst) in enumerate(((win_hbm, win), (wout_hbm, wout))):
        copy = pltpu.make_async_copy(src.at[0], dst, wsem.at[i])
        copy.start()
        weights.append(copy)

    barrier = pltpu.get_barrier_semaphore()
    peers = [{"expert": yh * HALF + t} for t in row[1:]] + [partner, up, down, side]
    for peer in peers:
        pl.semaphore_signal(barrier, inc=1, device_id=peer, device_id_type=MESH)

    def slots(j, routes, values):
        expert = lax.broadcasted_iota(jnp.int32, (HALF, toks), 0) + yh * HALF
        member = jnp.zeros((HALF, toks), F32)
        weight = jnp.zeros((HALF, toks), F32)
        for k in range(routes.shape[0]):
            hit = routes[k : k + 1, :] == expert
            member = jnp.where(hit, 1.0, member)
            weight = jnp.where(hit, values[k : k + 1, :], weight)
        first = lax.broadcasted_iota(jnp.int32, (toks, toks), 0)
        before = first < lax.broadcasted_iota(jnp.int32, (toks, toks), 1)
        rank = mm(member.astype(BF), jnp.where(before, 1.0, 0.0).astype(BF), ((1,), (0,)))
        rank = jnp.where(member > 0.0, rank, -1.0)
        spot = lax.broadcasted_iota(jnp.int32, (HALF, CAP, toks), 1).astype(F32)
        match = spot == rank[:, None, :]
        onehot[j] = jnp.where(match, 1.0, 0.0).reshape(HALF * CAP, toks).astype(BF)
        scale = jnp.sum(jnp.where(match, weight[:, None, :], 0.0), axis=2, keepdims=True)
        return scale.reshape(HALF * CAP, 1)

    def gather(j, source, send, scale, start, stop):
        for c in range(start, stop, 256):
            value = mm(onehot[j], source[:, c : c + 256], ((1,), (0,)))
            if scale is not None:
                value = value * scale
            send[j, :, :, c : c + 256] = value.reshape(HALF, CAP, 256).astype(BF)

    own_gate = slots(0, routing, gates)
    gather(0, tok, stok, None, 0, width)
    with jax.named_scope("barrier"):
        pl.semaphore_wait(barrier, len(peers))

    given = []
    half = width // 2
    for i, (src, dst) in enumerate((
            (routing, prt), (gates, pgt), (tok.at[:, :half], ptok.at[:, :half]), (tok.at[:, half:], ptok.at[:, half:]),
            (cot, pcot))):
        copy = pltpu.make_async_remote_copy(
            src_ref=src, dst_ref=dst, send_sem=ps.at[i], recv_sem=pr.at[i], device_id=partner, device_id_type=MESH)
        copy.start()
        given.append(copy)

    tok_copies, cot_copies = [], []
    thalf = width // TOK_SPLIT

    def spread(send, recv, ssem, rsem, osem):
        for o in range(1, HALF):
            pltpu.make_async_remote_copy(
                src_ref=send(row[o]), dst_ref=recv(r), send_sem=ssem, recv_sem=rsem,
                device_id={"expert": yh * HALF + row[o]}, device_id_type=MESH).start()
        own = pltpu.make_async_copy(send(r), recv(r), osem)
        own.start()
        some = slice(0, HALF - 1)
        whole = pltpu.make_async_remote_copy(
            src_ref=send(some), dst_ref=recv(some), send_sem=ssem, recv_sem=rsem,
            device_id=partner, device_id_type=MESH)
        return whole, own

    def send_tok(j, k):
        span = pl.ds(k * thalf, thalf)
        i = j * TOK_SPLIT + k
        tok_copies.append(spread(
            lambda t: stok.at[j, t, :, span], lambda t: rtok.at[j, t, :, span], ts.at[i], tr.at[i], lsem.at[i]))

    def send_cot(b):
        span = pl.ds(b * cblock, cblock)
        cot_copies.append(spread(
            lambda t: scot.at[:, t, :, span], lambda t: rcot.at[:, t, :, span], cs.at[b], cr.at[b],
            lsem.at[2 * TOK_SPLIT + b]))

    def arrived(entry):
        with jax.named_scope("arrived"):
            whole, own = entry
            own.wait()
            whole.wait_recv()

    for k in range(TOK_SPLIT):
        send_tok(0, k)
    gather(0, cot, scot, own_gate, 0, width)
    with jax.named_scope("pmeta"):
        given[0].wait_recv()
        given[1].wait_recv()
    partner_gate = slots(1, prt, pgt)
    for k in range(TOK_SPLIT):
        with jax.named_scope("ptok"):
            given[2 + k].wait_recv()
        gather(1, ptok, stok, None, k * thalf, (k + 1) * thalf)
        send_tok(1, k)
    with jax.named_scope("pcot"):
        given[4].wait_recv()
    gather(1, pcot, scot, partner_gate, 0, width)
    send_cot(0)

    weights[0].wait()
    for j in (0, 1):
        for k in range(TOK_SPLIT):
            arrived(tok_copies[j * TOK_SPLIT + k])
        if j == 1:
            send_cot(1)
        rows = slice(j * HALF * CAP, (j + 1) * HALF * CAP)
        for t in range(0, HALF, 2):
            at = (j * HALF + t) * CAP
            tokf[at : at + 2 * CAP, :] = rtok[j, t : t + 2].astype(F32).reshape(2 * CAP, width).astype(BF)
        for n in range(0, ff, 256):
            value = mm(tokf[rows, :], win[:, n : n + 256], ((1,), (0,)))
            hid[rows, n : n + 256] = (value * jax.nn.sigmoid(value)).astype(BF)
            slope[rows, n : n + 256] = silu_slope(value)
    weights[1].wait()

    def out_block(b):
        arrived(cot_copies[b])
        if b + 2 < COT_SPLIT:
            send_cot(b + 2)
        span = slice(b * cblock, (b + 1) * cblock)
        for j in (0, 1):
            for t in range(0, HALF, 2):
                at = (j * HALF + t) * CAP
                cotb[at : at + 2 * CAP, :] = rcot[j, t : t + 2, :, span].astype(F32).reshape(2 * CAP, cblock).astype(BF)
        for m in range(0, ff, 384):
            value = mm(hid[:, m : m + 384], cotb[...], ((0,), (0,)))
            po[b, m // 384] = value.reshape(8, 48, cblock).astype(BF)
        so.begin(b)

    def back_block(b):
        span = slice(b * cblock, (b + 1) * cblock)
        for n in range(0, ff, 256):
            value = mm(cotb[...], wout[n : n + 256, span], ((1,), (1,)))
            if b > 0:
                value += back[:, n : n + 256]
            if b < COT_SPLIT - 1:
                back[:, n : n + 256] = value
            else:
                pgrad[:, n : n + 256] = (value * slope[:, n : n + 256]).astype(BF)

    def in_block(n):
        with jax.named_scope(f"part_in{n}"):
            for m in range(0, width, 640):
                value = mm(tokf[:, m : m + 640], pgrad[:, n * 256 : (n + 1) * 256], ((0,), (0,)))
                value = value.reshape(4, 160, 256).astype(BF)
                for i in (0, 1):
                    pi[2 * n + i, m // 1280, m % 1280 // 160 : m % 1280 // 160 + 4] = value[:, :, i * 128 : (i + 1) * 128]
        si.begin(2 * n)
        si.begin(2 * n + 1)

    todo = (out_block, back_block, in_block, so.advance, si.advance)
    for entry in PLAN:
        todo[entry // 10](entry % 10)
    for b in range(COT_SPLIT):
        so.finish(b)
    for u in range(IN_UNITS):
        si.finish(u)
    for whole, _ in tok_copies + cot_copies:
        whole.wait_send()
    for copy in given:
        copy.wait_send()


def body(tokens, routing, gates, cotangent, w_in, w_out):
    toks, width = tokens.shape
    ff = w_in.shape[2]
    cblock = width // COT_SPLIT
    iblock = ff // IN_UNITS
    vmem = pl.BlockSpec(memory_space=pltpu.VMEM)
    hbm = pl.BlockSpec(memory_space=pl.ANY)
    dma = pltpu.SemaphoreType.DMA
    topk = routing.shape[1]
    slot = (2, HALF, CAP, width)
    return pl.pallas_call(
        kernel,
        out_shape=(
            jax.ShapeDtypeStruct((1, width // 16, ff), F32),
            jax.ShapeDtypeStruct((1, ff // 16, width), F32),
        ),
        in_specs=[vmem, vmem, vmem, vmem, hbm, hbm],
        out_specs=(vmem, vmem),
        scratch_shapes=[
            pltpu.VMEM((width, ff), BF), pltpu.VMEM((ff, width), BF),
            pltpu.VMEM(slot, BF), pltpu.VMEM(slot, BF), pltpu.VMEM(slot, BF), pltpu.VMEM(slot, BF),
            pltpu.VMEM((ROWS, width), BF), pltpu.VMEM((ROWS, cblock), BF), pltpu.VMEM((2, ROWS // 2, toks), BF),
            pltpu.VMEM((topk, toks), jnp.int32), pltpu.VMEM((topk, toks), F32),
            pltpu.VMEM((toks, width), BF), pltpu.VMEM((toks, width), BF),
            pltpu.VMEM((ROWS, ff), F32), pltpu.VMEM((ROWS, ff), F32),
            pltpu.VMEM((ROWS, ff), BF), pltpu.VMEM((ROWS, ff), BF),
            pltpu.VMEM((COT_SPLIT, 2, RING, ff // 16, cblock), BF), pltpu.VMEM((IN_UNITS, 2, RING, width // 16, iblock), BF),
            pltpu.VMEM((COT_SPLIT, 2, RING, ff // 16, cblock), BF), pltpu.VMEM((IN_UNITS, 2, RING, width // 16, iblock), BF),
            pltpu.VMEM((COT_SPLIT, ff // 16, cblock), BF), pltpu.VMEM((COT_SPLIT, ff // 16, cblock), BF),
            pltpu.VMEM((IN_UNITS, width // 16, iblock), BF), pltpu.VMEM((IN_UNITS, width // 16, iblock), BF),
            dma((2,)), dma((2 * TOK_SPLIT + COT_SPLIT,)), dma((5,)), dma((5,)),
            dma((2 * TOK_SPLIT,)), dma((2 * TOK_SPLIT,)), dma((COT_SPLIT,)), dma((COT_SPLIT,)),
            dma((COT_SPLIT,)), dma((COT_SPLIT, 8)), dma((IN_UNITS,)), dma((IN_UNITS, 8)),
            dma((COT_SPLIT,)), dma((COT_SPLIT,)), dma((IN_UNITS,)), dma((IN_UNITS,)),
        ],
        compiler_params=pltpu.CompilerParams(
            collective_id=0, has_side_effects=True, vmem_limit_bytes=62 * 1024 * 1024
        ),
    )(routing.T, gates.T, tokens, cotangent, w_in, w_out)


def solution(mesh):
    rows = P(("dp", "expert"), None)
    in_specs = (rows, rows, rows, rows, P("expert", None, None), P("expert", None, None))
    out_specs = (P("expert", "dp", None), P("expert", "dp", None))
    return jax.shard_map(body, mesh=mesh, in_specs=in_specs, out_specs=out_specs, check_vma=False)
```

```python
import functools

import jax
import jax.numpy as jnp
from jax import lax
from jax.experimental import pallas as pl
from jax.experimental.pallas import tpu as pltpu
from jax.sharding import PartitionSpec as P

MESH = pl.DeviceIdType.MESH
BF = jnp.bfloat16
F32 = jnp.float32
NEX = 16
HALF = 8
CAP = 40
ROWS = NEX * CAP
COT_SPLIT = 5
TOK_SPLIT = 2
IN_UNITS = 6
RING = 8
OUT_MODES = "zzzzy"
IN_MODES = "zzzyyy"
PLAN = (
    0, 10, 30, 1, 11, 30, 31, 2, 12, 30, 31, 32, 3, 30, 13, 31, 32, 33, 4, 14, 20, 21, 22, 31, 32,
    33, 40, 41, 42, 32, 34, 33, 40, 41, 42, 34, 43, 33, 40, 41, 44, 42, 43, 34, 40, 41, 44, 45, 42,
    43, 34, 45, 44, 43, 34, 45, 44, 43, 45, 44, 45,
)


def silu_slope(values):
    sigma = jax.nn.sigmoid(values)
    return sigma * (1.0 + values * (1.0 - sigma))


def mm(a, b, dims):
    return lax.dot_general(a, b, (dims, ((), ())), preferred_element_type=F32)


class Sums:
    def __init__(self, modes, cols, out, refs, place):
        self.modes, self.cols, self.out = modes, cols, out
        self.part, self.land, self.ysend, self.yrecv, self.ssem, self.rsem, self.yss, self.yrs = refs
        self.yl, self.z, self.up, self.down, self.side = place
        self.todo = {}

    def hops(self, u, direction):
        return range(1, 5) if self.modes[u] == "z" or u % 2 == direction else range(2, 5)

    def target(self, direction, s):
        return lax.rem(self.z + (5 - s if direction == 0 else s - 5) + RING, RING)

    def piece(self, u, direction, s):
        if self.modes[u] == "y":
            return self.yl
        if s == 1:
            return 1 - self.yl if direction == 0 else self.yl
        return slice(None)

    def remote(self, src, dst, ssem, rsem, device):
        return pltpu.make_async_remote_copy(
            src_ref=src, dst_ref=dst, send_sem=ssem, recv_sem=rsem, device_id=device, device_id_type=MESH)

    def hop(self, u, direction, s):
        slot = direction * 4 + s - 1
        row = self.piece(u, direction, s)
        return self.remote(
            self.part.at[u, row, self.target(direction, s)], self.land.at[u, row, slot],
            self.ssem.at[u], self.rsem.at[u, slot], self.up if direction == 0 else self.down)

    def step(self, u, s):
        for direction in (0, 1):
            if s not in self.hops(u, direction):
                continue
            if s - 1 in self.hops(u, direction):
                self.hop(u, direction, s - 1).wait_recv()
                row = self.piece(u, direction, s - 1)
                at = self.target(direction, s)
                got = self.land[u, row, direction * 4 + s - 2].astype(F32)
                self.part[u, row, at] = (self.part[u, row, at].astype(F32) + got).astype(BF)
            self.hop(u, direction, s).start()

    def ycopy(self, u):
        if self.modes[u] == "y":
            source, target = self.part.at[u, 1 - self.yl], self.land.at[u, self.yl]
        else:
            source, target = self.ysend.at[u], self.yrecv.at[u]
        return self.remote(source, target, self.yss.at[u], self.yrs.at[u], self.side)

    def begin(self, u):
        if self.modes[u] == "y":
            self.ycopy(u).start()
            self.todo[u] = ["add", 2, 3, 4, "end"]
        else:
            self.step(u, 1)
            self.todo[u] = [2, 3, 4, "end"]

    def advance(self, u):
        stage = self.todo[u].pop(0)
        with jax.named_scope(f"{stage}u{u}{self.modes[u]}{self.cols}"):
            if stage == "add":
                self.ycopy(u).wait_recv()
                got = self.land[u, 1 - self.yl].astype(F32)
                self.part[u, self.yl] = (self.part[u, self.yl].astype(F32) + got).astype(BF)
                self.step(u, 1)
            elif stage == "end":
                self.end(u)
            else:
                self.step(u, stage)

    def end(self, u):
        span = slice(self.cols * u, self.cols * (u + 1))
        for direction in (0, 1):
            self.hop(u, direction, 4).wait_recv()
        for row in (1 - self.yl, self.yl) if self.modes[u] == "z" else (self.yl,):
            total = self.part[u, row, self.z].astype(F32)
            total += self.land[u, row, 3].astype(F32) + self.land[u, row, 7].astype(F32)
            if self.modes[u] == "z" and row is not self.yl:
                self.ysend[u] = total.astype(BF)
                self.ycopy(u).start()
            else:
                self.out[0, :, span] = total

    def finish(self, u):
        assert not self.todo[u]
        span = slice(self.cols * u, self.cols * (u + 1))
        copy = self.ycopy(u)
        copy.wait_send()
        sent = slice(0, RING - 1)
        if self.modes[u] == "z":
            copy.wait_recv()
            self.out[0, :, span] += self.yrecv[u].astype(F32)
            all_sent = self.part.at[u, :, sent]
        else:
            all_sent = self.part.at[u, 0, sent]
        self.remote(all_sent, all_sent, self.ssem.at[u], self.rsem.at[u, 0], self.up).wait_send()


def kernel(routing, gates, tok, cot, win_hbm, wout_hbm, gin, gout,
           win, wout, stok, scot, rtok, rcot, tokf, cotb, onehot, prt, pgt, ptok, pcot, slope, back, hid, pgrad,
           po, pi, lo, li, yso, yro, ysi, yri,
           wsem, lsem, ps, pr, ts, tr, cs, cr, zos, zor, zis, zir, yos, yor, yis, yir):
    me = lax.axis_index("expert")
    dp = lax.axis_index("dp")
    yh = me // HALF
    r = lax.rem(me, HALF)
    yl = dp // RING
    z = lax.rem(dp, RING)
    up = {"dp": yl * RING + lax.rem(z + 1, RING)}
    down = {"dp": yl * RING + lax.rem(z + RING - 1, RING)}
    side = {"dp": (1 - yl) * RING + z}
    partner = {"expert": (1 - yh) * HALF + r}
    row = [lax.rem(r + o, HALF) for o in range(HALF)]
    width = tok.shape[1]
    toks = tok.shape[0]
    ff = win.shape[1]
    cblock = width // COT_SPLIT
    iblock = ff // IN_UNITS
    place = (yl, z, up, down, side)
    so = Sums(OUT_MODES, cblock, gout, (po, lo, yso, yro, zos, zor, yos, yor), place)
    si = Sums(IN_MODES, iblock, gin, (pi, li, ysi, yri, zis, zir, yis, yir), place)

    weights = []
    for i, (src, dst) in enumerate(((win_hbm, win), (wout_hbm, wout))):
        copy = pltpu.make_async_copy(src.at[0], dst, wsem.at[i])
        copy.start()
        weights.append(copy)

    barrier = pltpu.get_barrier_semaphore()
    peers = [{"expert": yh * HALF + t} for t in row[1:]] + [partner, up, down, side]
    for peer in peers:
        pl.semaphore_signal(barrier, inc=1, device_id=peer, device_id_type=MESH)

    def slots(j, routes, values):
        expert = lax.broadcasted_iota(jnp.int32, (HALF, toks), 0) + yh * HALF
        member = jnp.zeros((HALF, toks), F32)
        weight = jnp.zeros((HALF, toks), F32)
        for k in range(routes.shape[0]):
            hit = routes[k : k + 1, :] == expert
            member = jnp.where(hit, 1.0, member)
            weight = jnp.where(hit, values[k : k + 1, :], weight)
        first = lax.broadcasted_iota(jnp.int32, (toks, toks), 0)
        before = first < lax.broadcasted_iota(jnp.int32, (toks, toks), 1)
        rank = mm(member.astype(BF), jnp.where(before, 1.0, 0.0).astype(BF), ((1,), (0,)))
        rank = jnp.where(member > 0.0, rank, -1.0)
        spot = lax.broadcasted_iota(jnp.int32, (HALF, CAP, toks), 1).astype(F32)
        match = spot == rank[:, None, :]
        onehot[j] = jnp.where(match, 1.0, 0.0).reshape(HALF * CAP, toks).astype(BF)
        scale = jnp.sum(jnp.where(match, weight[:, None, :], 0.0), axis=2, keepdims=True)
        return scale.reshape(HALF * CAP, 1)

    def gather(j, source, send, scale, start, stop):
        for c in range(start, stop, 256):
            value = mm(onehot[j], source[:, c : c + 256], ((1,), (0,)))
            if scale is not None:
                value = value * scale
            send[j, :, :, c : c + 256] = value.reshape(HALF, CAP, 256).astype(BF)

    own_gate = slots(0, routing, gates)
    gather(0, tok, stok, None, 0, width)
    with jax.named_scope("barrier"):
        pl.semaphore_wait(barrier, len(peers))

    given = []
    half = width // 2
    for i, (src, dst) in enumerate((
            (routing, prt), (gates, pgt), (tok.at[:, :half], ptok.at[:, :half]), (tok.at[:, half:], ptok.at[:, half:]),
            (cot, pcot))):
        copy = pltpu.make_async_remote_copy(
            src_ref=src, dst_ref=dst, send_sem=ps.at[i], recv_sem=pr.at[i], device_id=partner, device_id_type=MESH)
        copy.start()
        given.append(copy)

    tok_copies, cot_copies = [], []
    thalf = width // TOK_SPLIT

    def spread(send, recv, ssem, rsem, osem):
        for o in range(1, HALF):
            pltpu.make_async_remote_copy(
                src_ref=send(row[o]), dst_ref=recv(r), send_sem=ssem, recv_sem=rsem,
                device_id={"expert": yh * HALF + row[o]}, device_id_type=MESH).start()
        own = pltpu.make_async_copy(send(r), recv(r), osem)
        own.start()
        some = slice(0, HALF - 1)
        whole = pltpu.make_async_remote_copy(
            src_ref=send(some), dst_ref=recv(some), send_sem=ssem, recv_sem=rsem,
            device_id=partner, device_id_type=MESH)
        return whole, own

    def send_tok(j, k):
        span = pl.ds(k * thalf, thalf)
        i = j * TOK_SPLIT + k
        tok_copies.append(spread(
            lambda t: stok.at[j, t, :, span], lambda t: rtok.at[j, t, :, span], ts.at[i], tr.at[i], lsem.at[i]))

    def send_cot(b):
        span = pl.ds(b * cblock, cblock)
        cot_copies.append(spread(
            lambda t: scot.at[:, t, :, span], lambda t: rcot.at[:, t, :, span], cs.at[b], cr.at[b],
            lsem.at[2 * TOK_SPLIT + b]))

    def arrived(entry):
        with jax.named_scope("arrived"):
            whole, own = entry
            own.wait()
            whole.wait_recv()

    for k in range(TOK_SPLIT):
        send_tok(0, k)
    gather(0, cot, scot, own_gate, 0, width)
    with jax.named_scope("pmeta"):
        given[0].wait_recv()
        given[1].wait_recv()
    partner_gate = slots(1, prt, pgt)
    for k in range(TOK_SPLIT):
        with jax.named_scope("ptok"):
            given[2 + k].wait_recv()
        gather(1, ptok, stok, None, k * thalf, (k + 1) * thalf)
        send_tok(1, k)
    with jax.named_scope("pcot"):
        given[4].wait_recv()
    gather(1, pcot, scot, partner_gate, 0, width)
    send_cot(0)

    weights[0].wait()
    for j in (0, 1):
        for k in range(TOK_SPLIT):
            arrived(tok_copies[j * TOK_SPLIT + k])
        if j == 1:
            send_cot(1)
        rows = slice(j * HALF * CAP, (j + 1) * HALF * CAP)
        for t in range(0, HALF, 2):
            at = (j * HALF + t) * CAP
            tokf[at : at + 2 * CAP, :] = rtok[j, t : t + 2].astype(F32).reshape(2 * CAP, width).astype(BF)
        for n in range(0, ff, 256):
            value = mm(tokf[rows, :], win[:, n : n + 256], ((1,), (0,)))
            hid[rows, n : n + 256] = (value * jax.nn.sigmoid(value)).astype(BF)
            slope[rows, n : n + 256] = silu_slope(value)
    weights[1].wait()

    def out_block(b):
        arrived(cot_copies[b])
        if b + 2 < COT_SPLIT:
            send_cot(b + 2)
        span = slice(b * cblock, (b + 1) * cblock)
        for j in (0, 1):
            for t in range(0, HALF, 2):
                at = (j * HALF + t) * CAP
                cotb[at : at + 2 * CAP, :] = rcot[j, t : t + 2, :, span].astype(F32).reshape(2 * CAP, cblock).astype(BF)
        for m in range(0, ff, 384):
            value = mm(hid[:, m : m + 384], cotb[...], ((0,), (0,)))
            po[b, m // 384] = value.reshape(8, 48, cblock).astype(BF)
        so.begin(b)

    def back_block(b):
        span = slice(b * cblock, (b + 1) * cblock)
        for n in range(0, ff, 256):
            value = mm(cotb[...], wout[n : n + 256, span], ((1,), (1,)))
            if b > 0:
                value += back[:, n : n + 256]
            if b < COT_SPLIT - 1:
                back[:, n : n + 256] = value
            else:
                pgrad[:, n : n + 256] = (value * slope[:, n : n + 256]).astype(BF)

    def in_block(n):
        with jax.named_scope(f"part_in{n}"):
            for m in range(0, width, 640):
                value = mm(tokf[:, m : m + 640], pgrad[:, n * 256 : (n + 1) * 256], ((0,), (0,)))
                value = value.reshape(4, 160, 256).astype(BF)
                for i in (0, 1):
                    pi[2 * n + i, m // 1280, m % 1280 // 160 : m % 1280 // 160 + 4] = value[:, :, i * 128 : (i + 1) * 128]
        si.begin(2 * n)
        si.begin(2 * n + 1)

    todo = (out_block, back_block, in_block, so.advance, si.advance)
    for entry in PLAN:
        todo[entry // 10](entry % 10)
    for b in range(COT_SPLIT):
        so.finish(b)
    for u in range(IN_UNITS):
        si.finish(u)
    for whole, _ in tok_copies + cot_copies:
        whole.wait_send()
    for copy in given:
        copy.wait_send()


def hand_over(a_in, b_in, a_out, b_out, a_buf, b_buf, sem):
    trips = []
    for i, (src, buf, dst) in enumerate(((a_in, a_buf, a_out), (b_in, b_buf, b_out))):
        into = pltpu.make_async_copy(src, buf, sem.at[2 * i])
        into.start()
        trips.append((into, pltpu.make_async_copy(buf, dst, sem.at[2 * i + 1])))
    for into, back in trips:
        into.wait()
        back.start()
    for _, back in trips:
        back.wait()


def body(tokens, routing, gates, cotangent, w_in, w_out):
    toks, width = tokens.shape
    ff = w_in.shape[2]
    cblock = width // COT_SPLIT
    iblock = ff // IN_UNITS
    vmem = pl.BlockSpec(memory_space=pltpu.VMEM)
    hbm = pl.BlockSpec(memory_space=pl.ANY)
    dma = pltpu.SemaphoreType.DMA
    topk = routing.shape[1]
    slot = (2, HALF, CAP, width)
    sums = pl.pallas_call(
        kernel,
        out_shape=(
            jax.ShapeDtypeStruct((1, width // 16, ff), F32),
            jax.ShapeDtypeStruct((1, ff // 16, width), F32),
        ),
        in_specs=[vmem, vmem, vmem, vmem, hbm, hbm],
        out_specs=(vmem, vmem),
        scratch_shapes=[
            pltpu.VMEM((width, ff), BF), pltpu.VMEM((ff, width), BF),
            pltpu.VMEM(slot, BF), pltpu.VMEM(slot, BF), pltpu.VMEM(slot, BF), pltpu.VMEM(slot, BF),
            pltpu.VMEM((ROWS, width), BF), pltpu.VMEM((ROWS, cblock), BF), pltpu.VMEM((2, ROWS // 2, toks), BF),
            pltpu.VMEM((topk, toks), jnp.int32), pltpu.VMEM((topk, toks), F32),
            pltpu.VMEM((toks, width), BF), pltpu.VMEM((toks, width), BF),
            pltpu.VMEM((ROWS, ff), F32), pltpu.VMEM((ROWS, ff), F32),
            pltpu.VMEM((ROWS, ff), BF), pltpu.VMEM((ROWS, ff), BF),
            pltpu.VMEM((COT_SPLIT, 2, RING, ff // 16, cblock), BF), pltpu.VMEM((IN_UNITS, 2, RING, width // 16, iblock), BF),
            pltpu.VMEM((COT_SPLIT, 2, RING, ff // 16, cblock), BF), pltpu.VMEM((IN_UNITS, 2, RING, width // 16, iblock), BF),
            pltpu.VMEM((COT_SPLIT, ff // 16, cblock), BF), pltpu.VMEM((COT_SPLIT, ff // 16, cblock), BF),
            pltpu.VMEM((IN_UNITS, width // 16, iblock), BF), pltpu.VMEM((IN_UNITS, width // 16, iblock), BF),
            dma((2,)), dma((2 * TOK_SPLIT + COT_SPLIT,)), dma((5,)), dma((5,)),
            dma((2 * TOK_SPLIT,)), dma((2 * TOK_SPLIT,)), dma((COT_SPLIT,)), dma((COT_SPLIT,)),
            dma((COT_SPLIT,)), dma((COT_SPLIT, 8)), dma((IN_UNITS,)), dma((IN_UNITS, 8)),
            dma((COT_SPLIT,)), dma((COT_SPLIT,)), dma((IN_UNITS,)), dma((IN_UNITS,)),
        ],
        compiler_params=pltpu.CompilerParams(
            collective_id=0, has_side_effects=True, vmem_limit_bytes=62 * 1024 * 1024
        ),
    )(routing.T, gates.T, tokens, cotangent, w_in, w_out)
    return pl.pallas_call(
        hand_over,
        out_shape=tuple(jax.ShapeDtypeStruct(x.shape, x.dtype) for x in sums),
        in_specs=[hbm, hbm],
        out_specs=(hbm, hbm),
        scratch_shapes=[pltpu.VMEM(x.shape, x.dtype) for x in sums] + [dma((4,))],
    )(*sums)


def solution(mesh):
    rows = P(("dp", "expert"), None)
    in_specs = (rows, rows, rows, rows, P("expert", None, None), P("expert", None, None))
    out_specs = (P("expert", "dp", None), P("expert", "dp", None))
    return jax.shard_map(body, mesh=mesh, in_specs=in_specs, out_specs=out_specs, check_vma=False)
```

```python
import functools

import jax
import jax.numpy as jnp
from jax import lax
from jax.experimental import pallas as pl
from jax.experimental.pallas import tpu as pltpu
from jax.sharding import PartitionSpec as P

MESH = pl.DeviceIdType.MESH
BF = jnp.bfloat16
F32 = jnp.float32
NEX = 16
HALF = 8
CAP = 40
ROWS = NEX * CAP
COT_SPLIT = 5
TOK_SPLIT = 2
IN_UNITS = 6
RING = 8
OUT_MODES = "zzzzz"
IN_MODES = "zzzyyy"
PLAN = (
    0, 10, 30, 1, 11, 30, 31, 2, 12, 30, 31, 32, 3, 30, 13, 31, 32, 33, 4, 14, 20, 21, 22, 31, 32,
    33, 34, 40, 41, 42, 32, 33, 43, 34, 40, 41, 42, 44, 33, 43, 34, 40, 45, 41, 42, 44, 43, 34, 40,
    45, 41, 42, 44, 43, 45, 44, 43, 45, 44, 45,
)


def silu_slope(values):
    sigma = jax.nn.sigmoid(values)
    return sigma * (1.0 + values * (1.0 - sigma))


def mm(a, b, dims):
    return lax.dot_general(a, b, (dims, ((), ())), preferred_element_type=F32)


class Sums:
    def __init__(self, modes, cols, out, refs, place):
        self.modes, self.cols, self.out = modes, cols, out
        self.part, self.land, self.ysend, self.yrecv, self.ssem, self.rsem, self.yss, self.yrs = refs
        self.yl, self.z, self.up, self.down, self.side = place
        self.todo = {}

    def hops(self, u, direction):
        return range(1, 5) if self.modes[u] == "z" or u % 2 == direction else range(2, 5)

    def target(self, direction, s):
        return lax.rem(self.z + (5 - s if direction == 0 else s - 5) + RING, RING)

    def piece(self, u, direction, s):
        if self.modes[u] == "y":
            return self.yl
        if s == 1:
            return 1 - self.yl if direction == 0 else self.yl
        return slice(None)

    def remote(self, src, dst, ssem, rsem, device):
        return pltpu.make_async_remote_copy(
            src_ref=src, dst_ref=dst, send_sem=ssem, recv_sem=rsem, device_id=device, device_id_type=MESH)

    def hop(self, u, direction, s):
        slot = direction * 4 + s - 1
        row = self.piece(u, direction, s)
        return self.remote(
            self.part.at[u, row, self.target(direction, s)], self.land.at[u, row, slot],
            self.ssem.at[u], self.rsem.at[u, slot], self.up if direction == 0 else self.down)

    def step(self, u, s):
        for direction in (0, 1):
            if s not in self.hops(u, direction):
                continue
            if s - 1 in self.hops(u, direction):
                self.hop(u, direction, s - 1).wait_recv()
                row = self.piece(u, direction, s - 1)
                at = self.target(direction, s)
                got = self.land[u, row, direction * 4 + s - 2].astype(F32)
                self.part[u, row, at] = (self.part[u, row, at].astype(F32) + got).astype(BF)
            self.hop(u, direction, s).start()

    def ycopy(self, u):
        if self.modes[u] == "y":
            source, target = self.part.at[u, 1 - self.yl], self.land.at[u, self.yl]
        else:
            source, target = self.ysend.at[u], self.yrecv.at[u]
        return self.remote(source, target, self.yss.at[u], self.yrs.at[u], self.side)

    def begin(self, u):
        if self.modes[u] == "y":
            self.ycopy(u).start()
            self.todo[u] = ["add", 2, 3, 4, "end"]
        else:
            self.step(u, 1)
            self.todo[u] = [2, 3, 4, "end"]

    def advance(self, u):
        stage = self.todo[u].pop(0)
        with jax.named_scope(f"{stage}u{u}{self.modes[u]}{self.cols}"):
            if stage == "add":
                self.ycopy(u).wait_recv()
                got = self.land[u, 1 - self.yl].astype(F32)
                self.part[u, self.yl] = (self.part[u, self.yl].astype(F32) + got).astype(BF)
                self.step(u, 1)
            elif stage == "end":
                self.end(u)
            else:
                self.step(u, stage)

    def end(self, u):
        span = slice(self.cols * u, self.cols * (u + 1))
        for direction in (0, 1):
            self.hop(u, direction, 4).wait_recv()
        for row in (1 - self.yl, self.yl) if self.modes[u] == "z" else (self.yl,):
            total = self.part[u, row, self.z].astype(F32)
            total += self.land[u, row, 3].astype(F32) + self.land[u, row, 7].astype(F32)
            if self.modes[u] == "z" and row is not self.yl:
                self.ysend[u] = total.astype(BF)
                self.ycopy(u).start()
            else:
                self.out[0, :, span] = total

    def finish(self, u):
        assert not self.todo[u]
        span = slice(self.cols * u, self.cols * (u + 1))
        copy = self.ycopy(u)
        copy.wait_send()
        sent = slice(0, RING - 1)
        if self.modes[u] == "z":
            copy.wait_recv()
            self.out[0, :, span] += self.yrecv[u].astype(F32)
            all_sent = self.part.at[u, :, sent]
        else:
            all_sent = self.part.at[u, 0, sent]
        self.remote(all_sent, all_sent, self.ssem.at[u], self.rsem.at[u, 0], self.up).wait_send()


def kernel(routing, gates, tok, cot, win_hbm, wout_hbm, gin, gout,
           win, wout, stok, scot, rtok, rcot, tokf, cotb, onehot, prt, pgt, ptok, pcot, slope, back, hid, pgrad,
           po, pi, lo, li, yso, yro, ysi, yri,
           wsem, lsem, ps, pr, ts, tr, cs, cr, zos, zor, zis, zir, yos, yor, yis, yir):
    me = lax.axis_index("expert")
    dp = lax.axis_index("dp")
    yh = me // HALF
    r = lax.rem(me, HALF)
    yl = dp // RING
    z = lax.rem(dp, RING)
    up = {"dp": yl * RING + lax.rem(z + 1, RING)}
    down = {"dp": yl * RING + lax.rem(z + RING - 1, RING)}
    side = {"dp": (1 - yl) * RING + z}
    partner = {"expert": (1 - yh) * HALF + r}
    row = [lax.rem(r + o, HALF) for o in range(HALF)]
    width = tok.shape[1]
    toks = tok.shape[0]
    ff = win.shape[1]
    cblock = width // COT_SPLIT
    iblock = ff // IN_UNITS
    place = (yl, z, up, down, side)
    so = Sums(OUT_MODES, cblock, gout, (po, lo, yso, yro, zos, zor, yos, yor), place)
    si = Sums(IN_MODES, iblock, gin, (pi, li, ysi, yri, zis, zir, yis, yir), place)

    weights = []
    for i, (src, dst) in enumerate(((win_hbm, win), (wout_hbm, wout))):
        copy = pltpu.make_async_copy(src.at[0], dst, wsem.at[i])
        copy.start()
        weights.append(copy)

    barrier = pltpu.get_barrier_semaphore()
    peers = [{"expert": yh * HALF + t} for t in row[1:]] + [partner, up, down, side]
    for peer in peers:
        pl.semaphore_signal(barrier, inc=1, device_id=peer, device_id_type=MESH)

    def slots(j, routes, values):
        expert = lax.broadcasted_iota(jnp.int32, (HALF, toks), 0) + yh * HALF
        member = jnp.zeros((HALF, toks), F32)
        weight = jnp.zeros((HALF, toks), F32)
        for k in range(routes.shape[0]):
            hit = routes[k : k + 1, :] == expert
            member = jnp.where(hit, 1.0, member)
            weight = jnp.where(hit, values[k : k + 1, :], weight)
        first = lax.broadcasted_iota(jnp.int32, (toks, toks), 0)
        before = first < lax.broadcasted_iota(jnp.int32, (toks, toks), 1)
        rank = mm(member.astype(BF), jnp.where(before, 1.0, 0.0).astype(BF), ((1,), (0,)))
        rank = jnp.where(member > 0.0, rank, -1.0)
        spot = lax.broadcasted_iota(jnp.int32, (HALF, CAP, toks), 1).astype(F32)
        match = spot == rank[:, None, :]
        onehot[j] = jnp.where(match, 1.0, 0.0).reshape(HALF * CAP, toks).astype(BF)
        scale = jnp.sum(jnp.where(match, weight[:, None, :], 0.0), axis=2, keepdims=True)
        return scale.reshape(HALF * CAP, 1)

    def gather(j, source, send, scale, start, stop):
        for c in range(start, stop, 256):
            value = mm(onehot[j], source[:, c : c + 256], ((1,), (0,)))
            if scale is not None:
                value = value * scale
            send[j, :, :, c : c + 256] = value.reshape(HALF, CAP, 256).astype(BF)

    own_gate = slots(0, routing, gates)
    gather(0, tok, stok, None, 0, width)
    with jax.named_scope("barrier"):
        pl.semaphore_wait(barrier, len(peers))

    given = []
    half = width // 2
    for i, (src, dst) in enumerate((
            (routing, prt), (gates, pgt), (tok.at[:, :half], ptok.at[:, :half]), (tok.at[:, half:], ptok.at[:, half:]),
            (cot, pcot))):
        copy = pltpu.make_async_remote_copy(
            src_ref=src, dst_ref=dst, send_sem=ps.at[i], recv_sem=pr.at[i], device_id=partner, device_id_type=MESH)
        copy.start()
        given.append(copy)

    tok_copies, cot_copies = [], []
    thalf = width // TOK_SPLIT

    def spread(send, recv, ssem, rsem, osem):
        for o in range(1, HALF):
            pltpu.make_async_remote_copy(
                src_ref=send(row[o]), dst_ref=recv(r), send_sem=ssem, recv_sem=rsem,
                device_id={"expert": yh * HALF + row[o]}, device_id_type=MESH).start()
        own = pltpu.make_async_copy(send(r), recv(r), osem)
        own.start()
        some = slice(0, HALF - 1)
        whole = pltpu.make_async_remote_copy(
            src_ref=send(some), dst_ref=recv(some), send_sem=ssem, recv_sem=rsem,
            device_id=partner, device_id_type=MESH)
        return whole, own

    def send_tok(j, k):
        span = pl.ds(k * thalf, thalf)
        i = j * TOK_SPLIT + k
        tok_copies.append(spread(
            lambda t: stok.at[j, t, :, span], lambda t: rtok.at[j, t, :, span], ts.at[i], tr.at[i], lsem.at[i]))

    def send_cot(b):
        span = pl.ds(b * cblock, cblock)
        cot_copies.append(spread(
            lambda t: scot.at[:, t, :, span], lambda t: rcot.at[:, t, :, span], cs.at[b], cr.at[b],
            lsem.at[2 * TOK_SPLIT + b]))

    def arrived(entry):
        with jax.named_scope("arrived"):
            whole, own = entry
            own.wait()
            whole.wait_recv()

    for k in range(TOK_SPLIT):
        send_tok(0, k)
    gather(0, cot, scot, own_gate, 0, width)
    with jax.named_scope("pmeta"):
        given[0].wait_recv()
        given[1].wait_recv()
    partner_gate = slots(1, prt, pgt)
    for k in range(TOK_SPLIT):
        with jax.named_scope("ptok"):
            given[2 + k].wait_recv()
        gather(1, ptok, stok, None, k * thalf, (k + 1) * thalf)
        send_tok(1, k)
    with jax.named_scope("pcot"):
        given[4].wait_recv()
    gather(1, pcot, scot, partner_gate, 0, width)
    send_cot(0)

    weights[0].wait()
    for j in (0, 1):
        for k in range(TOK_SPLIT):
            arrived(tok_copies[j * TOK_SPLIT + k])
        if j == 1:
            send_cot(1)
        rows = slice(j * HALF * CAP, (j + 1) * HALF * CAP)
        for t in range(0, HALF, 2):
            at = (j * HALF + t) * CAP
            tokf[at : at + 2 * CAP, :] = rtok[j, t : t + 2].astype(F32).reshape(2 * CAP, width).astype(BF)
        for n in range(0, ff, 256):
            value = mm(tokf[rows, :], win[:, n : n + 256], ((1,), (0,)))
            hid[rows, n : n + 256] = (value * jax.nn.sigmoid(value)).astype(BF)
            slope[rows, n : n + 256] = silu_slope(value)
    weights[1].wait()

    def out_block(b):
        arrived(cot_copies[b])
        if b + 2 < COT_SPLIT:
            send_cot(b + 2)
        span = slice(b * cblock, (b + 1) * cblock)
        for j in (0, 1):
            for t in range(0, HALF, 2):
                at = (j * HALF + t) * CAP
                cotb[at : at + 2 * CAP, :] = rcot[j, t : t + 2, :, span].astype(F32).reshape(2 * CAP, cblock).astype(BF)
        for m in range(0, ff, 384):
            value = mm(hid[:, m : m + 384], cotb[...], ((0,), (0,)))
            po[b, m // 384] = value.reshape(8, 48, cblock).astype(BF)
        so.begin(b)

    def back_block(b):
        span = slice(b * cblock, (b + 1) * cblock)
        for n in range(0, ff, 256):
            value = mm(cotb[...], wout[n : n + 256, span], ((1,), (1,)))
            if b > 0:
                value += back[:, n : n + 256]
            if b < COT_SPLIT - 1:
                back[:, n : n + 256] = value
            else:
                pgrad[:, n : n + 256] = (value * slope[:, n : n + 256]).astype(BF)

    def in_block(n):
        with jax.named_scope(f"part_in{n}"):
            for m in range(0, width, 640):
                value = mm(tokf[:, m : m + 640], pgrad[:, n * 256 : (n + 1) * 256], ((0,), (0,)))
                value = value.reshape(4, 160, 256).astype(BF)
                for i in (0, 1):
                    pi[2 * n + i, m // 1280, m % 1280 // 160 : m % 1280 // 160 + 4] = value[:, :, i * 128 : (i + 1) * 128]
        si.begin(2 * n)
        si.begin(2 * n + 1)

    todo = (out_block, back_block, in_block, so.advance, si.advance)
    for entry in PLAN:
        todo[entry // 10](entry % 10)
    for b in range(COT_SPLIT):
        so.finish(b)
    for u in range(IN_UNITS):
        si.finish(u)
    for whole, _ in tok_copies + cot_copies:
        whole.wait_send()
    for copy in given:
        copy.wait_send()


def hand_over(a_in, b_in, a_out, b_out, a_buf, b_buf, sem):
    trips = []
    for i, (src, buf, dst) in enumerate(((a_in, a_buf, a_out), (b_in, b_buf, b_out))):
        into = pltpu.make_async_copy(src, buf, sem.at[2 * i])
        into.start()
        trips.append((into, pltpu.make_async_copy(buf, dst, sem.at[2 * i + 1])))
    for into, back in trips:
        into.wait()
        back.start()
    for _, back in trips:
        back.wait()


def body(tokens, routing, gates, cotangent, w_in, w_out):
    toks, width = tokens.shape
    ff = w_in.shape[2]
    cblock = width // COT_SPLIT
    iblock = ff // IN_UNITS
    vmem = pl.BlockSpec(memory_space=pltpu.VMEM)
    hbm = pl.BlockSpec(memory_space=pl.ANY)
    dma = pltpu.SemaphoreType.DMA
    topk = routing.shape[1]
    slot = (2, HALF, CAP, width)
    sums = pl.pallas_call(
        kernel,
        out_shape=(
            jax.ShapeDtypeStruct((1, width // 16, ff), F32),
            jax.ShapeDtypeStruct((1, ff // 16, width), F32),
        ),
        in_specs=[vmem, vmem, vmem, vmem, hbm, hbm],
        out_specs=(vmem, vmem),
        scratch_shapes=[
            pltpu.VMEM((width, ff), BF), pltpu.VMEM((ff, width), BF),
            pltpu.VMEM(slot, BF), pltpu.VMEM(slot, BF), pltpu.VMEM(slot, BF), pltpu.VMEM(slot, BF),
            pltpu.VMEM((ROWS, width), BF), pltpu.VMEM((ROWS, cblock), BF), pltpu.VMEM((2, ROWS // 2, toks), BF),
            pltpu.VMEM((topk, toks), jnp.int32), pltpu.VMEM((topk, toks), F32),
            pltpu.VMEM((toks, width), BF), pltpu.VMEM((toks, width), BF),
            pltpu.VMEM((ROWS, ff), F32), pltpu.VMEM((ROWS, ff), F32),
            pltpu.VMEM((ROWS, ff), BF), pltpu.VMEM((ROWS, ff), BF),
            pltpu.VMEM((COT_SPLIT, 2, RING, ff // 16, cblock), BF), pltpu.VMEM((IN_UNITS, 2, RING, width // 16, iblock), BF),
            pltpu.VMEM((COT_SPLIT, 2, RING, ff // 16, cblock), BF), pltpu.VMEM((IN_UNITS, 2, RING, width // 16, iblock), BF),
            pltpu.VMEM((COT_SPLIT, ff // 16, cblock), BF), pltpu.VMEM((COT_SPLIT, ff // 16, cblock), BF),
            pltpu.VMEM((IN_UNITS, width // 16, iblock), BF), pltpu.VMEM((IN_UNITS, width // 16, iblock), BF),
            dma((2,)), dma((2 * TOK_SPLIT + COT_SPLIT,)), dma((5,)), dma((5,)),
            dma((2 * TOK_SPLIT,)), dma((2 * TOK_SPLIT,)), dma((COT_SPLIT,)), dma((COT_SPLIT,)),
            dma((COT_SPLIT,)), dma((COT_SPLIT, 8)), dma((IN_UNITS,)), dma((IN_UNITS, 8)),
            dma((COT_SPLIT,)), dma((COT_SPLIT,)), dma((IN_UNITS,)), dma((IN_UNITS,)),
        ],
        compiler_params=pltpu.CompilerParams(
            collective_id=0, has_side_effects=True, vmem_limit_bytes=62 * 1024 * 1024
        ),
    )(routing.T, gates.T, tokens, cotangent, w_in, w_out)
    return pl.pallas_call(
        hand_over,
        out_shape=tuple(jax.ShapeDtypeStruct(x.shape, x.dtype) for x in sums),
        in_specs=[hbm, hbm],
        out_specs=(hbm, hbm),
        scratch_shapes=[pltpu.VMEM(x.shape, x.dtype) for x in sums] + [dma((4,))],
    )(*sums)


def solution(mesh):
    rows = P(("dp", "expert"), None)
    in_specs = (rows, rows, rows, rows, P("expert", None, None), P("expert", None, None))
    out_specs = (P("expert", "dp", None), P("expert", "dp", None))
    return jax.shard_map(body, mesh=mesh, in_specs=in_specs, out_specs=out_specs, check_vma=False)
```
